768 devices in a mesh: grp: 24 (over x, z_lo, core), freq: 32 (over y, z_hi).
Axes of the slice: x: 4, y: 8, z: 12 (z_hi: 4, z_lo: 3; z = z_hi * 3 + z_lo), core: 2. Of those that a mesh axis runs over, the one named last changes fastest.
Arguments:
- spectra: float32 [192, 2, 4096], P('grp', None, 'freq'), may hold values from -6 to 6
- station_mask: int32 [192], P('grp'), may hold values 0 or 1
- owners: int32 [24, 2, 64, 1], P('grp'), may hold values from 0 to 23; in each aligned block of 64 rows (0 to 63, 64 to 127, ..., all dimensions but the last counted through in order) at most 6 rows name the same one
Outputs:
- inbox: float32 [24, 2, 24, 6, 4096], P('grp', None, None, None, 'freq')
The draws below stay inside these ranges and needn't reach their ends.
Inputs may be any that keep to these rules, and one draw needn't show every extreme that they name: `owners`: in each round, no owner is named by more than 6 of one group's 64 pairs, a bound that some block reaches; every group owns some pair.
All inputs are finite; a program needn't handle non-finite values. No bound on the sum of `station_mask` on one device may be relied on, other than what follows from the above.
Results may differ from the reference program's by a relative error of at most 0.0003.
Values sent between devices are 32-bit elements; how exact they have to be, the bound alone decides.
A program may use at most 32 MiB of HBM per device.

```python
import math
import jax
import jax.numpy as jnp
import numpy as np
from jax import lax

NF = 4096
LAGS = 4096
STA_DEV = 8
ROUNDS = 2
GROUPS = 24
STATIONS = 192
PAIRS = 64
CAP = 6


def set_ends(entries, own_key, low, top_value):
    extent = entries.shape
    index_at = [jax.random.randint(jax.random.fold_in(own_key, axis), (), 0, extent[axis]) for axis in range(len(extent))]
    entries = entries.at[tuple(index_at)].set(low)
    longest = extent.index(max(extent))
    index_at[longest] = (index_at[longest] + 1) % extent[longest]
    return entries.at[tuple(index_at)].set(top_value)


def steps_of(own_key, dims, split, smallest, largest):
    loudness, own = 1.0, jax.random.fold_in(own_key, 6)
    for axis_at, parts in split:
        draws = jnp.exp(jax.random.uniform(jax.random.fold_in(own, axis_at), (parts,), jnp.float32, smallest / len(split), largest / len(split)))
        loudness = loudness * jnp.repeat(draws, dims[axis_at] // parts).reshape([-1 if axis == axis_at else 1 for axis in range(len(dims))])
    return loudness


def shared_out(stream_key, own, number, rows, amount, top, most, skew):
    sequence = jax.random.permutation(stream_key, amount)
    heavy_load, usual = portions_of(amount, rows * top, most, skew, True), portions_of(amount, rows * top, most, skew, False)
    places = jnp.arange(amount)

    def named(tallies, rotation):
        used = int((tallies > 0).sum())
        fixed = max(1, used // 4)
        passed = fixed + (places - fixed + rotation * (used - fixed)) % max(1, amount - fixed)
        return jnp.zeros((amount,), jnp.int32).at[sequence[jnp.where(places < fixed, places, passed)]].set(jnp.asarray(tallies, jnp.int32))

    tallies = jnp.where(number % 4 == 0, named(heavy_load, number // 4), named(usual, number - number // 4 - 1))
    mixed = jax.random.permutation(jax.random.fold_in(own, 3), amount)
    giver, receiver = mixed[0:amount // 2 * 2:2], mixed[1:amount // 2 * 2:2]
    slack = jnp.minimum(tallies[giver] - 1, most - tallies[receiver]) // 2
    slack = jnp.where((giver == sequence[0]) | (receiver == sequence[0]) | (tallies[receiver] == 0), 0, jnp.maximum(slack, 0))
    passed = jax.random.randint(jax.random.fold_in(own, 4), (amount // 2,), 0, 1 << 20) % (slack + 1)
    tallies = tallies.at[giver].add(-passed).at[receiver].add(passed)
    members = jnp.searchsorted(jnp.cumsum(tallies), jnp.arange(rows * top), side="right").astype(jnp.int32)
    listing = members.reshape(top, rows).T
    listing = listing[jax.random.permutation(jax.random.fold_in(own, 1), rows)]
    rotation = jax.random.randint(jax.random.fold_in(own, 2), (rows, 1), 0, top)
    return jnp.take_along_axis(listing, (jnp.arange(top)[None, :] + rotation) % top, axis=1)


def portions_of(number_of, total, reach, slope, full):
    weights = [(1 << 20) // math.isqrt(grade ** slope) + 1 for grade in range(1, number_of + 1)]
    largest = reach if full else min(reach, max(-(-total // number_of), total * weights[0] // sum(weights)))
    least = 1 if total - largest >= number_of - 1 else 0
    counts, rest = [largest] + [least] * (number_of - 1), total - largest - least * (number_of - 1)
    while rest > 0:
        movable = [i for i in range(1, number_of) if counts[i] < largest] or [i for i in range(1, number_of) if counts[i] < reach]
        pool, remaining = sum([weights[i] for i in movable]), rest
        for i in movable:
            extra = min(reach - counts[i], max(1, remaining * weights[i] // pool), rest)
            counts[i] = counts[i] + extra
            rest = rest - extra
    return np.array(counts)


def noise(own_key, dims, width, limit, shards=(), kind=jnp.bfloat16):
    result = jax.random.normal(own_key, dims, jnp.float32) * width
    if len(shards) > 0:
        result = steps_of(own_key, dims, shards, -0.22, 0.18) * result
    return jnp.clip(result, min=-limit, max=limit).astype(kind)


def setup_inputs(seed: int = 0) -> dict:
    splits = jax.random.split(jax.random.key(seed), 4)
    spectra = noise(splits[0], (STATIONS, 2, NF), 1.0, 6.0, ((0, 24), (2, 32)), jnp.float32)
    station_mask = set_ends((jax.random.randint(splits[1], (STATIONS,), 0, 8) < 7).astype(jnp.int32), jax.random.fold_in(splits[1], 1), 0, 1)
    owners_keys = jax.random.split(jax.random.fold_in(splits[2], 1), GROUPS * ROUNDS * PAIRS // PAIRS)
    owners_turns = jax.random.permutation(jax.random.fold_in(splits[2], 3), GROUPS * ROUNDS * PAIRS // PAIRS)
    owners = jax.vmap(lambda own, number: shared_out(jax.random.fold_in(splits[2], 2), own, number, PAIRS, GROUPS, 1, CAP, 2))(owners_keys, owners_turns).reshape((GROUPS, ROUNDS, PAIRS, 1))
    return {"spectra": spectra, "station_mask": station_mask, "owners": owners}


def lag_tables(first_bin, bin_block):
    bin_ids = first_bin + jnp.arange(bin_block, dtype=jnp.int32)
    lag_ids = jnp.arange(LAGS, dtype=jnp.int32) - LAGS // 2
    phase_turns = jnp.mod(bin_ids[:, None] * lag_ids[None, :], 2 * NF)
    angles = phase_turns.astype(jnp.float32) * (math.pi / NF)
    return (jnp.cos(angles), jnp.sin(angles))

def to_lags(cross_real, cross_imag):
    bin_block = math.gcd(NF, 512)

    def accumulate(running, first_bin):
        cosine_table, sine_table = lag_tables(first_bin, bin_block)
        part_real = lax.dynamic_slice_in_dim(cross_real, first_bin, bin_block, 1)
        part_imag = lax.dynamic_slice_in_dim(cross_imag, first_bin, bin_block, 1)
        running = running + jnp.dot(part_real, cosine_table, precision=lax.Precision.HIGHEST)
        running = running - jnp.dot(part_imag, sine_table, precision=lax.Precision.HIGHEST)
        return (running, None)
    starts = jnp.arange(0, NF, bin_block, dtype=jnp.int32)
    running, _ = lax.scan(accumulate, jnp.zeros((cross_real.shape[0], LAGS), jnp.float32), starts)
    return running / math.sqrt(NF)

def reference(spectra, station_mask, owners):
    grouped = spectra.reshape(GROUPS, STA_DEV, 2, NF)
    weights = station_mask.reshape(GROUPS, STA_DEV).astype(jnp.float32)
    pair_ids = jnp.arange(PAIRS, dtype=jnp.int32)
    earlier = pair_ids[None, :] < pair_ids[:, None]
    slot_ids = jnp.arange(GROUPS * CAP, dtype=jnp.int32)
    results = []
    for round_index in range(ROUNDS):
        shift_by = round_index + 1
        partner = jnp.roll(grouped, shift_by, axis=0)
        partner_weight = jnp.roll(weights, shift_by, axis=0)
        pair_weight = (weights[:, :, None] * partner_weight[:, None, :])[..., None]
        cross_real = (grouped[:, :, None, 0] * partner[:, None, :, 0] + grouped[:, :, None, 1] * partner[:, None, :, 1]) * pair_weight
        cross_imag = (grouped[:, :, None, 1] * partner[:, None, :, 0] - grouped[:, :, None, 0] * partner[:, None, :, 1]) * pair_weight
        correlation = to_lags(cross_real.reshape(GROUPS * PAIRS, NF), cross_imag.reshape(GROUPS * PAIRS, NF))
        correlation = correlation.reshape(GROUPS, PAIRS, LAGS)
        owner_ids = owners[:, round_index, :, 0]
        same_owner = (owner_ids[:, :, None] == owner_ids[:, None, :]) & earlier[None]
        pair_rank = lax.optimization_barrier(jnp.sum(same_owner.astype(jnp.int32), axis=2))
        slot_index = owner_ids * CAP + pair_rank
        placing = (slot_index[:, :, None] == slot_ids[None, None, :]).astype(jnp.float32)
        received = jnp.einsum('gpx,gpl->gxl', placing, correlation, precision=lax.Precision.HIGHEST)
        results.append(received.reshape(GROUPS, GROUPS, CAP, LAGS))
    stacked = jnp.stack(results, axis=0)
    return jnp.transpose(stacked, (2, 0, 1, 3, 4))
```

```python
import functools
import math

import jax
import jax.numpy as jnp
from jax import lax
from jax.experimental import pallas as pl
from jax.experimental.pallas import tpu as pltpu
from jax.sharding import PartitionSpec as P

LAGS_PER = 128
STA = 8
PAIRS = STA * STA
ROUNDS = 2
ZH = 4
MESH = pl.DeviceIdType.MESH
F32 = jnp.float32
BF16 = jnp.bfloat16


def split(v):
    hi = v.astype(BF16)
    return hi, (v - hi.astype(F32)).astype(BF16)


def kernel(
    dims, x_ref, slot_ref, cos_ref, sin_ref, out_ref,
    buf, tab, xb, acc, sbuf, rbuf,
    own_sem, z_send, z_recv, y_send, y_recv, f_send, f_recv, a_send, a_recv,
):
    G, Y, Z, cap, capp = dims
    BINS = 128
    HALF = Z * BINS
    g = lax.axis_index("grp")
    f = lax.axis_index("freq")
    y = f // Z
    zh = lax.rem(f, Z)
    right = lax.rem(g + 1, G)

    def zpeer(d):
        return (g, y * Z + lax.rem(zh + d, Z))

    def ypeer(d):
        return (g, lax.rem(y + d, Y) * Z + zh)

    def gpeer(d):
        return (lax.rem(g + d, G), f)

    barrier = pltpu.get_barrier_semaphore()
    for d in range(1, Z):
        pl.semaphore_signal(barrier, inc=1, device_id=zpeer(d), device_id_type=MESH)

    @pl.loop(1, Y)
    def _(d):
        pl.semaphore_signal(barrier, inc=1, device_id=ypeer(d), device_id_type=MESH)

    @pl.loop(1, G)
    def _(d):
        pl.semaphore_signal(barrier, inc=1, device_id=gpeer(d), device_id_type=MESH)

    def rel(s):
        return jnp.where(lax.rem(s, 2) == 1, (s + 1) // 2, lax.rem(Y - s // 2, Y))

    base_cos = cos_ref[0:BINS, :]
    base_sin = sin_ref[0:BINS, :]

    @pl.loop(0, Y)
    def _(s):
        first = BINS + lax.rem(y + rel(s), Y) * Z
        for j in range(Z):
            ec = cos_ref[pl.ds(first + j, 1), :]
            es = sin_ref[pl.ds(first + j, 1), :]
            c = base_cos * ec - base_sin * es
            n = -(base_sin * ec + base_cos * es)
            rows = pl.ds(j * BINS, BINS)
            hi, lo = split(c)
            tab[s, rows, 0:LAGS_PER] = hi
            tab[s, rows, LAGS_PER:2 * LAGS_PER] = lo
            rows = pl.ds(HALF + j * BINS, BINS)
            hi, lo = split(n)
            tab[s, rows, 0:LAGS_PER] = hi
            tab[s, rows, LAGS_PER:2 * LAGS_PER] = lo

    pl.semaphore_wait(barrier, (Z - 1) + (Y - 1) + (G - 1))

    def z_copy(d):
        return pltpu.make_async_remote_copy(
            src_ref=x_ref, dst_ref=buf.at[0, y, zh],
            send_sem=z_send.at[d - 1], recv_sem=z_recv.at[d - 1],
            device_id=zpeer(d), device_id_type=MESH)

    def z_arrival(d):
        band = buf.at[0, y, lax.rem(zh + Z - d, Z)]
        return pltpu.make_async_remote_copy(
            src_ref=band, dst_ref=band,
            send_sem=z_send.at[d - 1], recv_sem=z_recv.at[d - 1],
            device_id=zpeer(d), device_id_type=MESH)

    def y_copy(d, j, src):
        return pltpu.make_async_remote_copy(
            src_ref=src, dst_ref=buf.at[0, y, lax.rem(zh + Z - d, Z)],
            send_sem=y_send.at[d, j], recv_sem=y_recv.at[d, j],
            device_id=ypeer(j), device_id_type=MESH)

    def y_arrival(d, row, j):
        band = buf.at[0, row, lax.rem(zh + Z - d, Z)]
        return pltpu.make_async_remote_copy(
            src_ref=band, dst_ref=band,
            send_sem=y_send.at[d, j], recv_sem=y_recv.at[d, j],
            device_id=ypeer(j), device_id_type=MESH)

    def f_copy(hop, s):
        row = lax.rem(y + rel(s), Y)
        return pltpu.make_async_remote_copy(
            src_ref=buf.at[hop, row], dst_ref=buf.at[hop + 1, row],
            send_sem=f_send.at[hop, s], recv_sem=f_recv.at[hop, s],
            device_id=(right, f), device_id_type=MESH)

    def a_copy(d):
        return pltpu.make_async_remote_copy(
            src_ref=sbuf.at[lax.rem(g + d, G)], dst_ref=rbuf.at[g],
            send_sem=a_send.at[d], recv_sem=a_recv.at[d],
            device_id=gpeer(d), device_id_type=MESH)

    own = pltpu.make_async_copy(x_ref, buf.at[0, y, zh], own_sem)
    own.start()
    order = sorted(range(1, Z), key=lambda d: -min(d, Z - d))
    for d in order:
        z_copy(d).start()
    for j in sorted(range(1, Y), key=lambda j: -min(j, Y - j)):
        y_copy(0, j, x_ref).start()
    acc[...] = jnp.zeros_like(acc)
    for d in reversed(order):
        z_arrival(d).wait_recv()
        src = buf.at[0, y, lax.rem(zh + Z - d, Z)]
        for j in sorted(range(1, Y), key=lambda j: -min(j, Y - j)):
            y_copy(d, j, src).start()
    own.wait()

    def product(s):
        row = lax.rem(y + rel(s), Y)
        for b in range(Z):
            are = buf[0, row, b, 0]
            aim = buf[0, row, b, 1]
            for r in range(ROUNDS):
                bre = buf[r + 1, row, b, 0][None, :, :]
                bim = buf[r + 1, row, b, 1][None, :, :]
                re = are[:, None, :] * bre + aim[:, None, :] * bim
                im = aim[:, None, :] * bre - are[:, None, :] * bim
                for part, v in ((0, re), (1, im)):
                    hi, lo = split(v.reshape(PAIRS, BINS))
                    cols = pl.ds(part * HALF + b * BINS, BINS)
                    xb[r * PAIRS:(r + 1) * PAIRS, cols] = hi
                    xb[(ROUNDS + r) * PAIRS:(ROUNDS + r + 1) * PAIRS, cols] = lo
        acc[...] += jnp.dot(xb[...], tab[s], preferred_element_type=F32)

    @pl.loop(0, Y + 2)
    def _(t):
        @pl.when((t > 0) & (t < Y))
        def _():
            row = lax.rem(y + rel(t), Y)
            j = Y - rel(t)
            for d in range(Z):
                y_arrival(d, row, j).wait_recv()

        @pl.when(t < Y)
        def _():
            f_copy(0, t).start()

        @pl.when((t >= 1) & (t <= Y))
        def _():
            f_copy(0, t - 1).wait_recv()
            f_copy(1, t - 1).start()

        @pl.when(t >= 2)
        def _():
            f_copy(1, t - 2).wait_recv()
            product(t - 2)

    whole = (acc[0:128, 0:128] + acc[0:128, 128:256]
             + acc[128:256, 0:128] + acc[128:256, 128:256])
    whole = whole * (1.0 / math.sqrt(Y * Z * BINS))
    hi, lo = split(whole)
    slots = lax.broadcasted_iota(jnp.int32, (G * capp, PAIRS), 0)
    for r in range(ROUNDS):
        place = jnp.where(slots == slot_ref[r:r + 1, :], 1.0, 0.0).astype(BF16)
        rows = slice(r * PAIRS, (r + 1) * PAIRS)
        got = jnp.dot(place, hi[rows], preferred_element_type=F32) + jnp.dot(
            place, lo[rows], preferred_element_type=F32)
        sbuf[:, r] = got.reshape(G, capp, LAGS_PER)

    @pl.loop(1, G)
    def _(d):
        a_copy(d).start()

    out_ref[0, :, g] = sbuf[g, :, 0:cap]

    for d in range(1, Z):
        z_copy(d).wait_send()

    @pl.loop(1, Y)
    def _(j):
        for d in range(Z):
            y_copy(d, j, x_ref).wait_send()

    @pl.loop(0, Y)
    def _(s):
        for hop in range(2):
            f_copy(hop, s).wait_send()

    @pl.loop(1, G)
    def _(d):
        src = lax.rem(g + G - d, G)
        block = rbuf.at[src]
        pltpu.make_async_remote_copy(
            src_ref=block, dst_ref=block,
            send_sem=a_send.at[d], recv_sem=a_recv.at[d],
            device_id=gpeer(d), device_id_type=MESH).wait_recv()
        out_ref[0, :, src] = rbuf[src, :, 0:cap]

    @pl.loop(1, G)
    def _(d):
        a_copy(d).wait_send()


def per_device(Z, spectra, station_mask, owners):
    G = lax.axis_size("grp")
    F = lax.axis_size("freq")
    Y = F // Z
    NF = F * 128
    cap = (2 * PAIRS + G - 1) // G
    capp = -(-cap // 8) * 8
    own = spectra.transpose(1, 0, 2) * station_mask.astype(F32)[None, :, None]
    ids = owners[0, :, :, 0]
    p = jnp.arange(PAIRS, dtype=jnp.int32)
    same = (ids[:, :, None] == ids[:, None, :]) & (p[:, None] < p[None, :])[None]
    slot = ids * capp + jnp.sum(same.astype(jnp.int32), axis=1)
    m = lax.axis_index("freq") * 128 + jnp.arange(128, dtype=jnp.int32) - NF // 2
    k = jnp.arange(128 + F, dtype=jnp.int32)
    k = jnp.where(k < 128, k, (k - 128) * 128)
    angle = jnp.mod(k[:, None] * m[None, :], 2 * NF).astype(F32) * (math.pi / NF)
    vm = pl.BlockSpec(memory_space=pltpu.VMEM)
    dma = pltpu.SemaphoreType.DMA
    return pl.pallas_call(
        functools.partial(kernel, (G, Y, Z, cap, capp)),
        out_shape=jax.ShapeDtypeStruct((1, ROUNDS, G, cap, 128), F32),
        in_specs=[vm] * 4,
        out_specs=vm,
        scratch_shapes=[
            pltpu.VMEM((ROUNDS + 1, Y, Z, 2, STA, 128), F32),
            pltpu.VMEM((Y, 2 * Z * 128, 256), BF16),
            pltpu.VMEM((256, 2 * Z * 128), BF16),
            pltpu.VMEM((256, 256), F32),
            pltpu.VMEM((G, ROUNDS, capp, 128), F32),
            pltpu.VMEM((G, ROUNDS, capp, 128), F32),
            dma, dma((Z - 1,)), dma((Z - 1,)),
            dma((Z, Y)), dma((Z, Y)),
            dma((2, Y)), dma((2, Y)),
            dma((G,)), dma((G,)),
        ],
        compiler_params=pltpu.CompilerParams(
            collective_id=0, has_side_effects=True, vmem_limit_bytes=32 << 20),
    )(own, slot, jnp.cos(angle), jnp.sin(angle))


def solution(mesh):
    placed = (P("grp", None, "freq"), P("grp"), P("grp", None, None, None))
    return jax.shard_map(
        functools.partial(per_device, ZH),
        mesh=mesh,
        in_specs=placed,
        out_specs=P("grp", None, None, None, "freq"),
        check_vma=False,
    )
```

```python
import functools
import math

import jax
import jax.numpy as jnp
from jax import lax
from jax.experimental import pallas as pl
from jax.experimental.pallas import tpu as pltpu
from jax.sharding import PartitionSpec as P

BINS = 128
STA = 8
PAIRS = STA * STA
ROUNDS = 2
Z = 4
CHIP_GROUPS = 6
UNITS = 2 * Z
PLACE = {1: 1, 3: 2, 2: 3}
MESH = pl.DeviceIdType.MESH
F32 = jnp.float32
BF16 = jnp.bfloat16


def split(v):
    hi = v.astype(BF16)
    return hi, (v - hi.astype(F32)).astype(BF16)


def trig(k, m, nf):
    angle = lax.rem(lax.rem(k * m, 2 * nf) + 2 * nf, 2 * nf).astype(F32) * (math.pi / nf)
    return jnp.cos(angle), jnp.sin(angle)


def kernel(
    dims, x_hbm, mask_hbm, owner_hbm, out_ref,
    xin, maskin, ownerin, place, phase, buf, tab, xb, acc, sbuf, rbuf,
    in_sem, z_send, z_recv, y_send, y_recv, f_send, f_recv, a_send, a_recv,
):
    G, Y, cap, capp = dims
    Q = Y // 2
    HALF = Q * BINS
    NF = Y * Z * BINS
    g = lax.axis_index("grp")
    f = lax.axis_index("freq")
    y = f // Z
    zh = lax.rem(f, Z)
    right = lax.rem(g + 1, G)
    per_x = CHIP_GROUPS if G % CHIP_GROUPS == 0 else 1
    X = G // per_x

    def zpeer(d):
        return (g, y * Z + lax.rem(zh + d, Z))

    def ypeer(d):
        return (g, lax.rem(y + d, Y) * Z + zh)

    def owner(i):
        turn = i // per_x
        dx = jnp.where(turn == X - 1, 0, lax.rem(X // 2 + jnp.where(
            lax.rem(turn, 2) == 1, X - (turn + 1) // 2, turn // 2), X))
        return lax.rem(g // per_x + dx, X) * per_x + lax.rem(i, per_x)

    barrier = pltpu.get_barrier_semaphore()

    def greet(peer):
        pl.semaphore_signal(barrier, inc=1, device_id=peer, device_id_type=MESH)

    greet(zpeer(1))
    greet(zpeer(Z - 1))

    @pl.loop(1, Y)
    def _(d):
        greet(ypeer(d))

    @pl.loop(1, G)
    def _(d):
        greet((lax.rem(g + d, G), f))

    loads = [
        pltpu.make_async_copy(a, b, in_sem.at[i])
        for i, (a, b) in enumerate(((x_hbm, xin), (mask_hbm, maskin), (owner_hbm, ownerin)))]
    for load in loads:
        load.start()

    lag = f * BINS + lax.broadcasted_iota(jnp.int32, (1, BINS), 1) - NF // 2
    base_cos, base_sin = trig(lax.broadcasted_iota(jnp.int32, (BINS, 1), 0), lag, NF)
    first_cos, first_sin = trig(
        BINS * lax.broadcasted_iota(jnp.int32, (Y * Z, 1), 0), lag, NF)
    phase[0] = first_cos
    phase[1] = first_sin
    for load in loads:
        load.wait()

    def column(row):
        n = row.shape[1]
        own = lax.broadcasted_iota(jnp.int32, (n, n), 0) == lax.broadcasted_iota(
            jnp.int32, (n, n), 1)
        return jnp.sum(jnp.where(own, row, 0.0), axis=1, keepdims=True)

    mask = column(maskin[...].astype(F32))
    buf[0, 0, 0, 0] = xin[:, 0, :] * mask
    buf[0, 0, 0, 1] = xin[:, 1, :] * mask
    for r in range(ROUNDS):
        row = ownerin[r:r + 1, :].astype(F32)
        ahead = lax.broadcasted_iota(jnp.int32, (PAIRS, PAIRS), 0) < lax.broadcasted_iota(
            jnp.int32, (PAIRS, PAIRS), 1)
        same = jnp.where(ahead & (column(row) == row), 1.0, 0.0)
        slot = row * capp + jnp.sum(same, axis=0, keepdims=True)
        slots = lax.broadcasted_iota(jnp.int32, (G * capp, PAIRS), 0).astype(F32)
        place[r] = jnp.where(slots == slot, 1.0, 0.0).astype(BF16)

    def rel(i):
        return jnp.where(lax.rem(i, 2) == 1, (i + 1) // 2, lax.rem(Y - i // 2, Y))

    @pl.loop(0, UNITS)
    def _(s):
        e = s // 2
        d = jnp.where(e == 2, 3, jnp.where(e == 3, 2, e))
        col = lax.rem(zh + Z - d, Z)
        for q in range(Q):
            band = lax.rem(y + rel(lax.rem(s, 2) * Q + q), Y) * Z + col
            ec = phase[0, pl.ds(band, 1), :]
            es = phase[1, pl.ds(band, 1), :]
            c = base_cos * ec - base_sin * es
            n = -(base_sin * ec + base_cos * es)
            for at, v in ((q * BINS, c), (HALF + q * BINS, n)):
                hi, lo = split(v)
                tab[s, at:at + BINS, 0:BINS] = hi
                tab[s, at:at + BINS, BINS:2 * BINS] = lo

    acc[...] = jnp.zeros_like(acc)
    pl.semaphore_wait(barrier, 2 + (Y - 1) + (G - 1))

    def remote(src, dst, ssem, rsem, peer):
        return pltpu.make_async_remote_copy(
            src_ref=src, dst_ref=dst, send_sem=ssem, recv_sem=rsem,
            device_id=peer, device_id_type=MESH)

    def z_copy(d):
        return remote(buf.at[0, 0, 0], buf.at[0, 2 * PLACE[d], 0],
                      z_send.at[PLACE[d] - 1], z_recv.at[PLACE[d] - 1], zpeer(d))

    def z_relay(d):
        part = 0 if d == 1 else 1
        return remote(buf.at[0, 2 * PLACE[d], 0, part], buf.at[0, 2 * PLACE[2], 0, part],
                      z_send.at[2 + part], z_recv.at[2 + part], zpeer(d))

    def y_copy(e, j):
        i = 2 * j if j < Y // 2 else 2 * (Y - j) - 1
        return remote(buf.at[0, 2 * e, 0], buf.at[0, 2 * e + i // Q, i % Q],
                      y_send.at[e, j], y_recv.at[e, i], ypeer(j))

    rows = sorted(range(1, Y), key=lambda j: -min(j, Y - j))

    def f_copy(hop, s):
        return remote(buf.at[hop, s], buf.at[hop + 1, s],
                      f_send.at[hop, s], f_recv.at[hop, s], (right, f))

    def a_copy(r, i):
        o = owner(i)
        return o, remote(sbuf.at[r, o], rbuf.at[r, g],
                         a_send.at[r, o], a_recv.at[r, g], (o, f))

    z_copy(1).start()
    z_copy(Z - 1).start()
    for j in rows:
        y_copy(0, j).start()
    for d in (1, Z - 1):
        z_copy(d).wait_recv()
        z_relay(d).start()
    for d in (1, Z - 1):
        for j in rows:
            y_copy(PLACE[d], j).start()

    def product(r, s):
        for q in range(Q):
            are = buf[0, s, q, 0]
            aim = buf[0, s, q, 1]
            bre = buf[r + 1, s, q, 0][None, :, :]
            bim = buf[r + 1, s, q, 1][None, :, :]
            re = are[:, None, :] * bre + aim[:, None, :] * bim
            im = aim[:, None, :] * bre - are[:, None, :] * bim
            for at, v in ((q * BINS, re), (HALF + q * BINS, im)):
                hi, lo = split(v.reshape(PAIRS, BINS))
                xb[0:PAIRS, at:at + BINS] = hi
                xb[PAIRS:2 * PAIRS, at:at + BINS] = lo
        acc[r] += jnp.dot(xb[...], tab[s], preferred_element_type=F32)

    def hand_out(r):
        whole = (acc[r, 0:PAIRS, 0:BINS] + acc[r, 0:PAIRS, BINS:2 * BINS]
                 + acc[r, PAIRS:2 * PAIRS, 0:BINS] + acc[r, PAIRS:2 * PAIRS, BINS:2 * BINS])
        hi, lo = split(whole * (1.0 / math.sqrt(NF)))
        got = jnp.dot(place[r], hi, preferred_element_type=F32) + jnp.dot(
            place[r], lo, preferred_element_type=F32)
        sbuf[r] = got.reshape(G, capp, BINS)

        @pl.loop(0, G)
        def _(i):
            o, copy = a_copy(r, i)

            @pl.when(o != g)
            def _():
                copy.start()

    @pl.loop(0, UNITS + 3)
    def _(t):
        @pl.when(t == 2)
        def _():
            for d in (1, Z - 1):
                z_relay(d).wait_recv()
            for j in rows:
                y_copy(PLACE[2], j).start()

        @pl.when(t < UNITS)
        def _():
            e = t // 2
            for q in range(Q):
                def arrive(q=q):
                    band = buf.at[0, t, q]
                    remote(band, band, y_send.at[0, 0],
                           y_recv.at[e, lax.rem(t, 2) * Q + q], (right, f)).wait_recv()
                if q == 0:
                    pl.when(lax.rem(t, 2) == 1)(arrive)
                else:
                    arrive()
            f_copy(0, t).start()

        @pl.when(t >= 3)
        def _():
            f_copy(0, t - 3).wait_recv()
            f_copy(1, t - 3).start()
            product(0, t - 3)

        @pl.when(t >= 5)
        def _():
            f_copy(1, t - 5).wait_recv()
            product(1, t - 5)

    hand_out(0)

    @pl.loop(UNITS - 2, UNITS)
    def _(s):
        f_copy(1, s).wait_recv()
        product(1, s)

    hand_out(1)
    for r in range(ROUNDS):
        out_ref[pl.ds(r * cap * G + g, cap, stride=G), :] = sbuf[r, g, 0:cap]

    for d in (1, Z - 1):
        z_copy(d).wait_send()
        z_relay(d).wait_send()
    for e in range(Z):
        for j in rows:
            y_copy(e, j).wait_send()

    @pl.loop(0, UNITS)
    def _(s):
        for hop in range(2):
            f_copy(hop, s).wait_send()

    for r in range(ROUNDS):
        @pl.loop(0, G)
        def _(src, r=r):
            @pl.when(src != g)
            def _():
                block = rbuf.at[r, src]
                copy = remote(block, block, a_send.at[r, src], a_recv.at[r, src], (src, f))
                copy.wait_recv()
                copy.wait_send()
                out_ref[pl.ds(r * cap * G + src, cap, stride=G), :] = rbuf[r, src, 0:cap]


def per_device(spectra, station_mask, owners):
    G = lax.axis_size("grp")
    F = lax.axis_size("freq")
    Y = F // Z
    cap = (2 * PAIRS + G - 1) // G
    capp = -(-cap // 8) * 8
    hbm = pl.BlockSpec(memory_space=pltpu.HBM)
    dma = pltpu.SemaphoreType.DMA
    vmem = pltpu.VMEM
    held = pl.pallas_call(
        functools.partial(kernel, (G, Y, cap, capp)),
        out_shape=jax.ShapeDtypeStruct((ROUNDS * cap * G, BINS), F32),
        in_specs=[hbm] * 3,
        out_specs=pl.BlockSpec(memory_space=vmem),
        scratch_shapes=[
            vmem((STA, 2, BINS), F32),
            vmem((1, STA), jnp.int32),
            vmem((ROUNDS, PAIRS), jnp.int32),
            vmem((ROUNDS, G * capp, PAIRS), BF16),
            vmem((2, F, BINS), F32),
            vmem((ROUNDS + 1, UNITS, Y // 2, 2, STA, BINS), F32),
            vmem((UNITS, Y * BINS, 2 * BINS), BF16),
            vmem((2 * PAIRS, Y * BINS), BF16),
            vmem((ROUNDS, 2 * PAIRS, 2 * BINS), F32),
            vmem((ROUNDS, G, capp, BINS), F32),
            vmem((ROUNDS, G, capp, BINS), F32),
            dma((3,)), dma((4,)), dma((4,)),
            dma((Z, Y)), dma((Z, Y)),
            dma((2, UNITS)), dma((2, UNITS)),
            dma((ROUNDS, G)), dma((ROUNDS, G)),
        ],
        compiler_params=pltpu.CompilerParams(
            collective_id=0, has_side_effects=True, vmem_limit_bytes=32 << 20),
    )(spectra, station_mask.reshape(1, STA), owners.reshape(ROUNDS, PAIRS))
    return held.reshape(1, ROUNDS, cap, G, BINS).transpose(0, 1, 3, 2, 4)


def solution(mesh):
    placed = (P("grp", None, "freq"), P("grp"), P("grp", None, None, None))
    return jax.shard_map(
        per_device,
        mesh=mesh,
        in_specs=placed,
        out_specs=P("grp", None, None, None, "freq"),
        check_vma=False,
    )
```

```python
import functools
import math

import jax
import jax.numpy as jnp
from jax import lax
from jax.experimental import pallas as pl
from jax.experimental.pallas import tpu as pltpu
from jax.sharding import PartitionSpec as P

BINS = 128
STA = 8
PAIRS = STA * STA
ROUNDS = 2
LAG = 4
Z = 4
CHIP_GROUPS = 6
UNITS = 2 * Z
PLACE = {1: 1, 3: 2, 2: 3}
MESH = pl.DeviceIdType.MESH
F32 = jnp.float32
BF16 = jnp.bfloat16


def split(v):
    hi = v.astype(BF16)
    return hi, (v - hi.astype(F32)).astype(BF16)


def trig(k, m, nf):
    angle = lax.rem(lax.rem(k * m, 2 * nf) + 2 * nf, 2 * nf).astype(F32) * (math.pi / nf)
    return jnp.cos(angle), jnp.sin(angle)


def kernel(
    dims, x_hbm, mask_hbm, owner_hbm, out_ref,
    xin, maskin, ownerin, place, phase, buf, tab, xb, acc, sbuf, rbuf,
    in_sem, z_send, z_recv, y_send, y_recv, f_send, f_recv, a_send, a_recv,
):
    G, Y, cap, capp = dims
    Q = Y // 2
    HALF = Q * BINS
    NF = Y * Z * BINS
    g = lax.axis_index("grp")
    f = lax.axis_index("freq")
    y = f // Z
    zh = lax.rem(f, Z)
    right = lax.rem(g + 1, G)
    per_x = CHIP_GROUPS if G % CHIP_GROUPS == 0 else 1
    X = G // per_x

    def zpeer(d):
        return (g, y * Z + lax.rem(zh + d, Z))

    def ypeer(d):
        return (g, lax.rem(y + d, Y) * Z + zh)

    turns = sorted(range(X), key=lambda dx: -min(dx, X - dx))
    mine = lax.rem(g, per_x)

    def along(dx, b):
        return lax.rem(g // per_x + dx, X) * per_x + b

    def other(o, dx, do):
        if dx == 0:
            pl.when(o != g)(do)
        else:
            do()

    barrier = pltpu.get_barrier_semaphore()

    def greet(peer):
        pl.semaphore_signal(barrier, inc=1, device_id=peer, device_id_type=MESH)

    greet(zpeer(1))
    greet(zpeer(Z - 1))

    @pl.loop(1, Y)
    def _(d):
        greet(ypeer(d))

    @pl.loop(1, G)
    def _(d):
        greet((lax.rem(g + d, G), f))

    loads = [
        pltpu.make_async_copy(a, b, in_sem.at[i])
        for i, (a, b) in enumerate(((x_hbm, xin), (mask_hbm, maskin), (owner_hbm, ownerin)))]
    for load in loads:
        load.start()

    for load in loads:
        load.wait()

    def column(row):
        n = row.shape[1]
        own = lax.broadcasted_iota(jnp.int32, (n, n), 0) == lax.broadcasted_iota(
            jnp.int32, (n, n), 1)
        return jnp.sum(jnp.where(own, row, 0.0), axis=1, keepdims=True)

    mask = column(maskin[...].astype(F32))
    buf[0, 0, 0, 0] = xin[:, 0, :] * mask
    buf[0, 0, 0, 1] = xin[:, 1, :] * mask
    def rel(i):
        return jnp.where(lax.rem(i, 2) == 1, (i + 1) // 2, lax.rem(Y - i // 2, Y))

    pl.semaphore_wait(barrier, 2 + (Y - 1) + (G - 1))

    def remote(src, dst, ssem, rsem, peer):
        return pltpu.make_async_remote_copy(
            src_ref=src, dst_ref=dst, send_sem=ssem, recv_sem=rsem,
            device_id=peer, device_id_type=MESH)

    def z_copy(d):
        return remote(buf.at[0, 0, 0], buf.at[0, 2 * PLACE[d], 0],
                      z_send.at[PLACE[d] - 1], z_recv.at[PLACE[d] - 1], zpeer(d))

    def z_relay(d):
        part = 0 if d == 1 else 1
        return remote(buf.at[0, 2 * PLACE[d], 0, part], buf.at[0, 2 * PLACE[2], 0, part],
                      z_send.at[2 + part], z_recv.at[2 + part], zpeer(d))

    def y_copy(e, j):
        i = 2 * j if j < Y // 2 else 2 * (Y - j) - 1
        return remote(buf.at[0, 2 * e, 0], buf.at[0, 2 * e + i // Q, i % Q],
                      y_send.at[e, j], y_recv.at[e, i], ypeer(j))

    rows = sorted(range(1, Y), key=lambda j: -min(j, Y - j))

    def f_copy(hop, s):
        return remote(buf.at[0, s], buf.at[hop + 1, s], f_send.at[hop, s],
                      f_recv.at[hop, s], (lax.rem(g + 1 + hop, G), f))

    def a_copy(dx, b):
        o = along(dx, b)
        return o, remote(sbuf.at[o], rbuf.at[g], a_send.at[dx * per_x + b],
                         a_recv.at[dx * per_x + mine], (o, f))

    z_copy(1).start()
    z_copy(Z - 1).start()
    for j in rows:
        y_copy(0, j).start()
    lag = f * BINS + lax.broadcasted_iota(jnp.int32, (1, BINS), 1) - NF // 2
    base_cos, base_sin = trig(lax.broadcasted_iota(jnp.int32, (BINS, 1), 0), lag, NF)
    first_cos, first_sin = trig(
        BINS * lax.broadcasted_iota(jnp.int32, (Y * Z, 1), 0), lag, NF)
    phase[0] = first_cos
    phase[1] = first_sin
    def table(s):
        e = s // 2
        d = jnp.where(e == 2, 3, jnp.where(e == 3, 2, e))
        col = lax.rem(zh + Z - d, Z)
        for q in range(Q):
            band = lax.rem(y + rel(lax.rem(s, 2) * Q + q), Y) * Z + col
            ec = phase[0, pl.ds(band, 1), :]
            es = phase[1, pl.ds(band, 1), :]
            c = base_cos * ec - base_sin * es
            n = -(base_sin * ec + base_cos * es)
            for at, v in ((q * BINS, c), (HALF + q * BINS, n)):
                hi, lo = split(v)
                tab[s, at:at + BINS, 0:BINS] = hi
                tab[s, at:at + BINS, BINS:2 * BINS] = lo

    pl.loop(0, UNITS // 2)(table)
    acc[...] = jnp.zeros_like(acc)
    for d in (1, Z - 1):
        z_copy(d).wait_recv()
        z_relay(d).start()
    for d in (1, Z - 1):
        for j in rows:
            y_copy(PLACE[d], j).start()
    pl.loop(UNITS // 2, UNITS)(table)

    for r in range(ROUNDS):
        row = ownerin[r:r + 1, :].astype(F32)
        ahead = lax.broadcasted_iota(jnp.int32, (PAIRS, PAIRS), 0) < lax.broadcasted_iota(
            jnp.int32, (PAIRS, PAIRS), 1)
        same = jnp.where(ahead & (column(row) == row), 1.0, 0.0)
        slot = row * capp + jnp.sum(same, axis=0, keepdims=True)
        slots = lax.broadcasted_iota(jnp.int32, (G * capp, PAIRS), 0).astype(F32)
        place[r] = jnp.where(slots == slot, 1.0, 0.0).astype(BF16)


    def product(s):
        for q in range(Q):
            are = buf[0, s, q, 0]
            aim = buf[0, s, q, 1]
            for r in range(ROUNDS):
                bre = buf[r + 1, s, q, 0][None, :, :]
                bim = buf[r + 1, s, q, 1][None, :, :]
                re = are[:, None, :] * bre + aim[:, None, :] * bim
                im = aim[:, None, :] * bre - are[:, None, :] * bim
                for at, v in ((q * BINS, re), (HALF + q * BINS, im)):
                    hi, lo = split(v.reshape(PAIRS, BINS))
                    xb[2 * r * PAIRS:(2 * r + 1) * PAIRS, at:at + BINS] = hi
                    xb[(2 * r + 1) * PAIRS:(2 * r + 2) * PAIRS, at:at + BINS] = lo
        acc[...] += jnp.dot(xb[...], tab[s], preferred_element_type=F32)

    @pl.loop(0, UNITS + LAG)
    def _(t):
        @pl.when(t == 2)
        def _():
            for d in (1, Z - 1):
                z_relay(d).wait_recv()
            for j in rows:
                y_copy(PLACE[2], j).start()

        @pl.when(t < UNITS)
        def _():
            e = t // 2
            for q in range(Q):
                def arrive(q=q):
                    band = buf.at[0, t, q]
                    remote(band, band, y_send.at[0, 0],
                           y_recv.at[e, lax.rem(t, 2) * Q + q], (right, f)).wait_recv()
                if q == 0:
                    pl.when(lax.rem(t, 2) == 1)(arrive)
                else:
                    arrive()
            f_copy(0, t).start()
            f_copy(1, t).start()

        @pl.when(t >= LAG)
        def _():
            f_copy(0, t - LAG).wait_recv()
            f_copy(1, t - LAG).wait_recv()
            product(t - LAG)

    for r in range(ROUNDS):
        top, low = 2 * r * PAIRS, (2 * r + 1) * PAIRS
        whole = (acc[top:low, 0:BINS] + acc[top:low, BINS:2 * BINS]
                 + acc[low:low + PAIRS, 0:BINS] + acc[low:low + PAIRS, BINS:2 * BINS])
        hi, lo = split(whole * (1.0 / math.sqrt(NF)))
        got = jnp.dot(place[r], hi, preferred_element_type=F32) + jnp.dot(
            place[r], lo, preferred_element_type=F32)
        sbuf[:, r] = got.reshape(G, capp, BINS)[:, 0:cap]
    for dx in turns:
        for b in range(per_x):
            o, copy = a_copy(dx, b)
            other(o, dx, copy.start)
    for r in range(ROUNDS):
        out_ref[pl.ds(r * cap * G + g, cap, stride=G), :] = sbuf[g, r]

    for d in (1, Z - 1):
        z_copy(d).wait_send()
        z_relay(d).wait_send()
    for e in range(Z):
        for j in rows:
            y_copy(e, j).wait_send()

    @pl.loop(0, UNITS)
    def _(s):
        for hop in range(2):
            f_copy(hop, s).wait_send()

    for dx in reversed(turns):
        for b in range(per_x):
            src = along(X - dx, b)

            def take(dx=dx, b=b, src=src):
                block = rbuf.at[src]
                remote(block, block, a_send.at[dx * per_x + b],
                       a_recv.at[dx * per_x + b], (src, f)).wait_recv()
                for r in range(ROUNDS):
                    out_ref[pl.ds(r * cap * G + src, cap, stride=G), :] = rbuf[src, r]

            other(src, dx, take)
    for dx in turns:
        for b in range(per_x):
            o, copy = a_copy(dx, b)
            other(o, dx, copy.wait_send)


def per_device(spectra, station_mask, owners):
    G = lax.axis_size("grp")
    F = lax.axis_size("freq")
    Y = F // Z
    cap = (2 * PAIRS + G - 1) // G
    capp = -(-cap // 8) * 8
    hbm = pl.BlockSpec(memory_space=pltpu.HBM)
    dma = pltpu.SemaphoreType.DMA
    vmem = pltpu.VMEM
    held = pl.pallas_call(
        functools.partial(kernel, (G, Y, cap, capp)),
        out_shape=jax.ShapeDtypeStruct((ROUNDS * cap * G, BINS), F32),
        in_specs=[hbm] * 3,
        out_specs=pl.BlockSpec(memory_space=vmem),
        scratch_shapes=[
            vmem((STA, 2, BINS), F32),
            vmem((1, STA), jnp.int32),
            vmem((ROUNDS, PAIRS), jnp.int32),
            vmem((ROUNDS, G * capp, PAIRS), BF16),
            vmem((2, F, BINS), F32),
            vmem((ROUNDS + 1, UNITS, Y // 2, 2, STA, BINS), F32),
            vmem((UNITS, Y * BINS, 2 * BINS), BF16),
            vmem((2 * ROUNDS * PAIRS, Y * BINS), BF16),
            vmem((2 * ROUNDS * PAIRS, 2 * BINS), F32),
            vmem((G, ROUNDS, cap, BINS), F32),
            vmem((G, ROUNDS, cap, BINS), F32),
            dma((3,)), dma((4,)), dma((4,)),
            dma((Z, Y)), dma((Z, Y)),
            dma((2, UNITS)), dma((2, UNITS)),
            dma((G,)), dma((G,)),
        ],
        compiler_params=pltpu.CompilerParams(
            collective_id=0, has_side_effects=True, vmem_limit_bytes=32 << 20),
    )(*(pltpu.with_memory_space_constraint(v, pltpu.HBM) for v in (spectra, station_mask.reshape(1, STA), owners.reshape(ROUNDS, PAIRS))))
    return held.reshape(1, ROUNDS, cap, G, BINS).transpose(0, 1, 3, 2, 4)


def solution(mesh):
    placed = (P("grp", None, "freq"), P("grp"), P("grp", None, None, None))
    return jax.shard_map(
        per_device,
        mesh=mesh,
        in_specs=placed,
        out_specs=P("grp", None, None, None, "freq"),
        check_vma=False,
    )
```

```python
import functools
import math

import jax
import jax.numpy as jnp
from jax import lax
from jax.experimental import pallas as pl
from jax.experimental.pallas import tpu as pltpu
from jax.sharding import PartitionSpec as P

BINS = 128
STA = 8
PAIRS = STA * STA
ROUNDS = 2
LAG = 4
Z = 4
CHIP_GROUPS = 6
UNITS = 2 * Z
PLACE = {1: 1, 3: 2, 2: 3}
MESH = pl.DeviceIdType.MESH
F32 = jnp.float32
BF16 = jnp.bfloat16


def split(v):
    hi = v.astype(BF16)
    return hi, (v - hi.astype(F32)).astype(BF16)


def trig(k, m, nf):
    angle = lax.rem(lax.rem(k * m, 2 * nf) + 2 * nf, 2 * nf).astype(F32) * (math.pi / nf)
    return jnp.cos(angle), jnp.sin(angle)


def kernel(
    dims, x_hbm, mask_hbm, owner_hbm, out_ref,
    xin, maskin, ownerin, place, phase, buf, tab, xb, acc, sbuf, rbuf,
    in_sem, z_send, z_recv, y_send, y_recv, f_send, f_recv, a_send, a_recv,
):
    G, Y, cap, capp = dims
    Q = Y // 2
    HALF = Q * BINS
    NF = Y * Z * BINS
    g = lax.axis_index("grp")
    f = lax.axis_index("freq")
    y = f // Z
    zh = lax.rem(f, Z)
    right = lax.rem(g + 1, G)
    per_x = CHIP_GROUPS if G % CHIP_GROUPS == 0 else 1
    X = G // per_x

    def zpeer(d):
        return (g, y * Z + lax.rem(zh + d, Z))

    def ypeer(d):
        return (g, lax.rem(y + d, Y) * Z + zh)

    turns = sorted(range(X), key=lambda dx: -min(dx, X - dx))
    mine = lax.rem(g, per_x)

    def along(dx, b):
        return lax.rem(g // per_x + dx, X) * per_x + b

    def other(o, dx, do):
        if dx == 0:
            pl.when(o != g)(do)
        else:
            do()

    loads = [
        pltpu.make_async_copy(a, b, in_sem.at[i])
        for i, (a, b) in enumerate(((x_hbm, xin), (mask_hbm, maskin), (owner_hbm, ownerin)))]
    for load in loads:
        load.start()

    barrier = pltpu.get_barrier_semaphore()

    def greet(peer):
        pl.semaphore_signal(barrier, inc=1, device_id=peer, device_id_type=MESH)

    greet(zpeer(1))
    greet(zpeer(Z - 1))

    @pl.loop(1, Y)
    def _(d):
        greet(ypeer(d))

    @pl.loop(1, G)
    def _(d):
        greet((lax.rem(g + d, G), f))


    for load in loads:
        load.wait()

    def column(row):
        n = row.shape[1]
        own = lax.broadcasted_iota(jnp.int32, (n, n), 0) == lax.broadcasted_iota(
            jnp.int32, (n, n), 1)
        return jnp.sum(jnp.where(own, row, 0.0), axis=1, keepdims=True)

    mask = column(maskin[...].astype(F32))
    buf[0, 0, 0, 0] = xin[:, 0, :] * mask
    buf[0, 0, 0, 1] = xin[:, 1, :] * mask
    def rel(i):
        return jnp.where(lax.rem(i, 2) == 1, (i + 1) // 2, lax.rem(Y - i // 2, Y))

    pl.semaphore_wait(barrier, 2 + (Y - 1) + (G - 1))

    def remote(src, dst, ssem, rsem, peer):
        return pltpu.make_async_remote_copy(
            src_ref=src, dst_ref=dst, send_sem=ssem, recv_sem=rsem,
            device_id=peer, device_id_type=MESH)

    def z_copy(d):
        return remote(buf.at[0, 0, 0], buf.at[0, 2 * PLACE[d], 0],
                      z_send.at[PLACE[d] - 1], z_recv.at[PLACE[d] - 1], zpeer(d))

    def z_relay():
        return remote(buf.at[0, 2 * PLACE[Z - 1], 0], buf.at[0, 2 * PLACE[2], 0],
                      z_send.at[2], z_recv.at[2], zpeer(Z - 1))

    def y_copy(e, j):
        i = 2 * j if j < Y // 2 else 2 * (Y - j) - 1
        return remote(buf.at[0, 2 * e, 0], buf.at[0, 2 * e + i // Q, i % Q],
                      y_send.at[e, j], y_recv.at[e, i], ypeer(j))

    rows = sorted(range(1, Y), key=lambda j: -min(j, Y - j))

    def f_copy(hop, s):
        return remote(buf.at[0, s], buf.at[hop + 1, s], f_send.at[hop, s],
                      f_recv.at[hop, s], (lax.rem(g + 1 + hop, G), f))

    def a_copy(dx, b):
        o = along(dx, b)
        return o, remote(sbuf.at[o], rbuf.at[g], a_send.at[dx * per_x + b],
                         a_recv.at[dx * per_x + mine], (o, f))

    z_copy(1).start()
    z_copy(Z - 1).start()
    for j in rows:
        y_copy(0, j).start()
    lag = f * BINS + lax.broadcasted_iota(jnp.int32, (1, BINS), 1) - NF // 2
    base_cos, base_sin = trig(lax.broadcasted_iota(jnp.int32, (BINS, 1), 0), lag, NF)
    first_cos, first_sin = trig(
        BINS * lax.broadcasted_iota(jnp.int32, (Y * Z, 1), 0), lag, NF)
    phase[0] = first_cos
    phase[1] = first_sin
    def table(s):
        e = s // 2
        d = jnp.where(e == 2, 3, jnp.where(e == 3, 2, e))
        col = lax.rem(zh + Z - d, Z)
        for q in range(Q):
            band = lax.rem(y + rel(lax.rem(s, 2) * Q + q), Y) * Z + col
            ec = phase[0, pl.ds(band, 1), :]
            es = phase[1, pl.ds(band, 1), :]
            c = base_cos * ec - base_sin * es
            n = -(base_sin * ec + base_cos * es)
            for at, v in ((q * BINS, c), (HALF + q * BINS, n)):
                hi, lo = split(v)
                tab[s, at:at + BINS, 0:BINS] = hi
                tab[s, at:at + BINS, BINS:2 * BINS] = lo

    pl.loop(0, UNITS // 2)(table)
    acc[...] = jnp.zeros_like(acc)
    z_copy(Z - 1).wait_recv()
    z_relay().start()
    z_copy(1).wait_recv()
    for d in (1, Z - 1):
        for j in rows:
            y_copy(PLACE[d], j).start()
    pl.loop(UNITS // 2, UNITS)(table)

    for r in range(ROUNDS):
        row = ownerin[r:r + 1, :].astype(F32)
        ahead = lax.broadcasted_iota(jnp.int32, (PAIRS, PAIRS), 0) < lax.broadcasted_iota(
            jnp.int32, (PAIRS, PAIRS), 1)
        same = jnp.where(ahead & (column(row) == row), 1.0, 0.0)
        slot = row * capp + jnp.sum(same, axis=0, keepdims=True)
        slots = lax.broadcasted_iota(jnp.int32, (G * capp, PAIRS), 0).astype(F32)
        place[r] = jnp.where(slots == slot, 1.0, 0.0).astype(BF16)


    def product(s):
        for q in range(Q):
            are = buf[0, s, q, 0]
            aim = buf[0, s, q, 1]
            for r in range(ROUNDS):
                bre = buf[r + 1, s, q, 0][None, :, :]
                bim = buf[r + 1, s, q, 1][None, :, :]
                re = are[:, None, :] * bre + aim[:, None, :] * bim
                im = aim[:, None, :] * bre - are[:, None, :] * bim
                for at, v in ((q * BINS, re), (HALF + q * BINS, im)):
                    hi, lo = split(v.reshape(PAIRS, BINS))
                    xb[2 * r * PAIRS:(2 * r + 1) * PAIRS, at:at + BINS] = hi
                    xb[(2 * r + 1) * PAIRS:(2 * r + 2) * PAIRS, at:at + BINS] = lo
        acc[...] += jnp.dot(xb[...], tab[s], preferred_element_type=F32)

    @pl.loop(0, UNITS + LAG + 1)
    def _(t):
        @pl.when(t == 2)
        def _():
            z_relay().wait_recv()
            for j in rows:
                y_copy(PLACE[2], j).start()

        @pl.when(t < UNITS)
        def _():
            e = t // 2
            for q in range(Q):
                def arrive(q=q):
                    band = buf.at[0, t, q]
                    remote(band, band, y_send.at[0, 0],
                           y_recv.at[e, lax.rem(t, 2) * Q + q], (right, f)).wait_recv()
                if q == 0:
                    pl.when(lax.rem(t, 2) == 1)(arrive)
                else:
                    arrive()
            f_copy(1, t).start()
            f_copy(0, t).start()

        @pl.when((t >= LAG) & (t != UNITS - 2))
        def _():
            u = t - LAG - jnp.where(t > UNITS - 2, 1, 0)
            f_copy(0, u).wait_recv()
            f_copy(1, u).wait_recv()
            product(u)

    for r in range(ROUNDS):
        top, low = 2 * r * PAIRS, (2 * r + 1) * PAIRS
        whole = (acc[top:low, 0:BINS] + acc[top:low, BINS:2 * BINS]
                 + acc[low:low + PAIRS, 0:BINS] + acc[low:low + PAIRS, BINS:2 * BINS])
        hi, lo = split(whole * (1.0 / math.sqrt(NF)))
        got = jnp.dot(place[r], hi, preferred_element_type=F32) + jnp.dot(
            place[r], lo, preferred_element_type=F32)
        sbuf[:, r] = got.reshape(G, capp, BINS)[:, 0:cap]
    for dx in turns:
        for b in range(per_x):
            o, copy = a_copy(dx, b)
            other(o, dx, copy.start)
    for r in range(ROUNDS):
        out_ref[pl.ds(r * cap * G + g, cap, stride=G), :] = sbuf[g, r]

    for d in (1, Z - 1):
        z_copy(d).wait_send()
    z_relay().wait_send()
    for e in range(Z):
        for j in rows:
            y_copy(e, j).wait_send()

    @pl.loop(0, UNITS)
    def _(s):
        for hop in range(2):
            f_copy(hop, s).wait_send()

    for dx in reversed(turns):
        for b in range(per_x):
            src = along(X - dx, b)

            def take(dx=dx, b=b, src=src):
                block = rbuf.at[src]
                remote(block, block, a_send.at[dx * per_x + b],
                       a_recv.at[dx * per_x + b], (src, f)).wait_recv()
                for r in range(ROUNDS):
                    out_ref[pl.ds(r * cap * G + src, cap, stride=G), :] = rbuf[src, r]

            other(src, dx, take)
    for dx in turns:
        for b in range(per_x):
            o, copy = a_copy(dx, b)
            other(o, dx, copy.wait_send)


def per_device(spectra, station_mask, owners):
    G = lax.axis_size("grp")
    F = lax.axis_size("freq")
    Y = F // Z
    cap = (2 * PAIRS + G - 1) // G
    capp = -(-cap // 8) * 8
    hbm = pl.BlockSpec(memory_space=pltpu.HBM)
    dma = pltpu.SemaphoreType.DMA
    vmem = pltpu.VMEM
    held = pl.pallas_call(
        functools.partial(kernel, (G, Y, cap, capp)),
        out_shape=jax.ShapeDtypeStruct((ROUNDS * cap * G, BINS), F32),
        in_specs=[hbm] * 3,
        out_specs=pl.BlockSpec(memory_space=vmem),
        scratch_shapes=[
            vmem((STA, 2, BINS), F32),
            vmem((1, STA), jnp.int32),
            vmem((ROUNDS, PAIRS), jnp.int32),
            vmem((ROUNDS, G * capp, PAIRS), BF16),
            vmem((2, F, BINS), F32),
            vmem((ROUNDS + 1, UNITS, Y // 2, 2, STA, BINS), F32),
            vmem((UNITS, Y * BINS, 2 * BINS), BF16),
            vmem((2 * ROUNDS * PAIRS, Y * BINS), BF16),
            vmem((2 * ROUNDS * PAIRS, 2 * BINS), F32),
            vmem((G, ROUNDS, cap, BINS), F32),
            vmem((G, ROUNDS, cap, BINS), F32),
            dma((3,)), dma((3,)), dma((3,)),
            dma((Z, Y)), dma((Z, Y)),
            dma((2, UNITS)), dma((2, UNITS)),
            dma((G,)), dma((G,)),
        ],
        compiler_params=pltpu.CompilerParams(
            collective_id=0, has_side_effects=True, vmem_limit_bytes=32 << 20),
    )(*(pltpu.with_memory_space_constraint(v, pltpu.HBM) for v in (spectra, station_mask.reshape(1, STA), owners.reshape(ROUNDS, PAIRS))))
    return held.reshape(1, ROUNDS, cap, G, BINS).transpose(0, 1, 3, 2, 4)


def solution(mesh):
    placed = (P("grp", None, "freq"), P("grp"), P("grp", None, None, None))
    return jax.shard_map(
        per_device,
        mesh=mesh,
        in_specs=placed,
        out_specs=P("grp", None, None, None, "freq"),
        check_vma=False,
    )
```

```python
import functools
import math

import jax
import jax.numpy as jnp
from jax import lax
from jax.experimental import pallas as pl
from jax.experimental.pallas import tpu as pltpu
from jax.sharding import PartitionSpec as P

BINS = 128
STA = 8
PAIRS = STA * STA
ROUNDS = 2
LAG = 4
Z = 4
CHIP_GROUPS = 6
UNITS = 2 * Z
PLACE = {1: 1, 3: 2, 2: 3}
MESH = pl.DeviceIdType.MESH
F32 = jnp.float32
BF16 = jnp.bfloat16


def split(v):
    hi = v.astype(BF16)
    return hi, (v - hi.astype(F32)).astype(BF16)


def trig(k, m, nf):
    angle = lax.rem(lax.rem(k * m, 2 * nf) + 2 * nf, 2 * nf).astype(F32) * (math.pi / nf)
    return jnp.cos(angle), jnp.sin(angle)


def kernel(
    dims, x_hbm, mask_hbm, owner_hbm, out_ref,
    xin, maskin, ownerin, place, phase, buf, tab, xb, acc, sbuf, rbuf,
    in_sem, z_send, z_recv, y_send, y_recv, f_send, f_recv, a_send, a_recv,
):
    G, Y, cap, capp = dims
    Q = Y // 2
    HALF = Q * BINS
    NF = Y * Z * BINS
    g = lax.axis_index("grp")
    f = lax.axis_index("freq")
    y = f // Z
    zh = lax.rem(f, Z)
    right = lax.rem(g + 1, G)
    per_x = CHIP_GROUPS if G % CHIP_GROUPS == 0 else 1
    X = G // per_x

    def zpeer(d):
        return (g, y * Z + lax.rem(zh + d, Z))

    def ypeer(d):
        return (g, lax.rem(y + d, Y) * Z + zh)

    turns = sorted(range(X), key=lambda dx: -min(dx, X - dx))
    mine = lax.rem(g, per_x)

    def along(dx, b):
        return lax.rem(g // per_x + dx, X) * per_x + b

    def other(o, dx, do):
        if dx == 0:
            pl.when(o != g)(do)
        else:
            do()

    loads = [
        pltpu.make_async_copy(a, b, in_sem.at[i])
        for i, (a, b) in enumerate(((x_hbm, xin), (mask_hbm, maskin), (owner_hbm, ownerin)))]
    for load in loads:
        load.start()

    barrier = pltpu.get_barrier_semaphore()

    def greet(peer):
        pl.semaphore_signal(barrier, inc=1, device_id=peer, device_id_type=MESH)

    greet(zpeer(1))
    greet(zpeer(Z - 1))

    @pl.loop(1, Y)
    def _(d):
        greet(ypeer(d))

    @pl.loop(1, G)
    def _(d):
        greet((lax.rem(g + d, G), f))


    for load in loads[:2]:
        load.wait()

    def column(row):
        n = row.shape[1]
        own = lax.broadcasted_iota(jnp.int32, (n, n), 0) == lax.broadcasted_iota(
            jnp.int32, (n, n), 1)
        return jnp.sum(jnp.where(own, row, 0.0), axis=1, keepdims=True)

    mask = column(maskin[...].astype(F32))
    buf[0, 0, 0, 0] = xin[:, 0, :] * mask
    buf[0, 0, 0, 1] = xin[:, 1, :] * mask
    def rel(i):
        return jnp.where(lax.rem(i, 2) == 1, (i + 1) // 2, lax.rem(Y - i // 2, Y))

    pl.semaphore_wait(barrier, 2 + (Y - 1) + (G - 1))

    def remote(src, dst, ssem, rsem, peer):
        return pltpu.make_async_remote_copy(
            src_ref=src, dst_ref=dst, send_sem=ssem, recv_sem=rsem,
            device_id=peer, device_id_type=MESH)

    def z_copy(d):
        return remote(buf.at[0, 0, 0], buf.at[0, 2 * PLACE[d], 0],
                      z_send.at[PLACE[d] - 1], z_recv.at[PLACE[d] - 1], zpeer(d))

    def z_relay():
        return remote(buf.at[0, 2 * PLACE[Z - 1], 0], buf.at[0, 2 * PLACE[2], 0],
                      z_send.at[2], z_recv.at[2], zpeer(Z - 1))

    def y_copy(e, j):
        i = 2 * j if j < Y // 2 else 2 * (Y - j) - 1
        return remote(buf.at[0, 2 * e, 0], buf.at[0, 2 * e + i // Q, i % Q],
                      y_send.at[e, j], y_recv.at[e, i], ypeer(j))

    rows = sorted(range(1, Y), key=lambda j: -min(j, Y - j))

    def f_copy(hop, s):
        return remote(buf.at[0, s], buf.at[hop + 1, s], f_send.at[hop, s],
                      f_recv.at[hop, s], (lax.rem(g + 1 + hop, G), f))

    def a_copy(dx, b):
        o = along(dx, b)
        return o, remote(sbuf.at[o], rbuf.at[g], a_send.at[dx * per_x + b],
                         a_recv.at[dx * per_x + mine], (o, f))

    z_copy(1).start()
    z_copy(Z - 1).start()
    for j in rows:
        y_copy(0, j).start()
    lag = f * BINS + lax.broadcasted_iota(jnp.int32, (1, BINS), 1) - NF // 2
    base_cos, base_sin = trig(lax.broadcasted_iota(jnp.int32, (BINS, 1), 0), lag, NF)
    first_cos, first_sin = trig(
        BINS * lax.broadcasted_iota(jnp.int32, (Y * Z, 1), 0), lag, NF)
    phase[0] = first_cos
    phase[1] = first_sin
    def table(s):
        e = s // 2
        d = jnp.where(e == 2, 3, jnp.where(e == 3, 2, e))
        col = lax.rem(zh + Z - d, Z)
        for q in range(Q):
            band = lax.rem(y + rel(lax.rem(s, 2) * Q + q), Y) * Z + col
            ec = phase[0, pl.ds(band, 1), :]
            es = phase[1, pl.ds(band, 1), :]
            c = base_cos * ec - base_sin * es
            n = -(base_sin * ec + base_cos * es)
            for at, v in ((q * BINS, c), (HALF + q * BINS, n)):
                hi, lo = split(v)
                tab[s, at:at + BINS, 0:BINS] = hi
                tab[s, at:at + BINS, BINS:2 * BINS] = lo

    pl.loop(0, UNITS // 2)(table)
    acc[...] = jnp.zeros_like(acc)
    z_copy(Z - 1).wait_recv()
    z_relay().start()
    z_copy(1).wait_recv()
    for d in (1, Z - 1):
        for j in rows:
            y_copy(PLACE[d], j).start()
    pl.loop(UNITS // 2, UNITS)(table)

    loads[2].wait()
    for r in range(ROUNDS):
        row = ownerin[r:r + 1, :].astype(F32)
        ahead = lax.broadcasted_iota(jnp.int32, (PAIRS, PAIRS), 0) < lax.broadcasted_iota(
            jnp.int32, (PAIRS, PAIRS), 1)
        same = jnp.where(ahead & (column(row) == row), 1.0, 0.0)
        slot = row * capp + jnp.sum(same, axis=0, keepdims=True)
        slots = lax.broadcasted_iota(jnp.int32, (G * capp, PAIRS), 0).astype(F32)
        place[r] = jnp.where(slots == slot, 1.0, 0.0).astype(BF16)


    def product(s):
        for q in range(Q):
            are = buf[0, s, q, 0]
            aim = buf[0, s, q, 1]
            for r in range(ROUNDS):
                bre = buf[r + 1, s, q, 0][None, :, :]
                bim = buf[r + 1, s, q, 1][None, :, :]
                re = are[:, None, :] * bre + aim[:, None, :] * bim
                im = aim[:, None, :] * bre - are[:, None, :] * bim
                for at, v in ((q * BINS, re), (HALF + q * BINS, im)):
                    hi, lo = split(v.reshape(PAIRS, BINS))
                    xb[2 * r * PAIRS:(2 * r + 1) * PAIRS, at:at + BINS] = hi
                    xb[(2 * r + 1) * PAIRS:(2 * r + 2) * PAIRS, at:at + BINS] = lo
        acc[...] += jnp.dot(xb[...], tab[s], preferred_element_type=F32)

    @pl.loop(0, UNITS + LAG + 1)
    def _(t):
        @pl.when(t == 2)
        def _():
            z_relay().wait_recv()
            for j in rows:
                y_copy(PLACE[2], j).start()

        @pl.when(t < UNITS)
        def _():
            e = t // 2
            for q in range(Q):
                def arrive(q=q):
                    band = buf.at[0, t, q]
                    remote(band, band, y_send.at[0, 0],
                           y_recv.at[e, lax.rem(t, 2) * Q + q], (right, f)).wait_recv()
                if q == 0:
                    pl.when(lax.rem(t, 2) == 1)(arrive)
                else:
                    arrive()
            f_copy(1, t).start()
            f_copy(0, t).start()

        @pl.when((t >= LAG) & (t != UNITS - 2))
        def _():
            u = t - LAG - jnp.where(t > UNITS - 2, 1, 0)
            f_copy(0, u).wait_recv()
            f_copy(1, u).wait_recv()
            product(u)

    for r in range(ROUNDS):
        top, low = 2 * r * PAIRS, (2 * r + 1) * PAIRS
        whole = (acc[top:low, 0:BINS] + acc[top:low, BINS:2 * BINS]
                 + acc[low:low + PAIRS, 0:BINS] + acc[low:low + PAIRS, BINS:2 * BINS])
        hi, lo = split(whole * (1.0 / math.sqrt(NF)))
        got = jnp.dot(place[r], hi, preferred_element_type=F32) + jnp.dot(
            place[r], lo, preferred_element_type=F32)
        sbuf[:, r] = got.reshape(G, capp, BINS)[:, 0:cap]
    for dx in turns:
        for b in range(per_x):
            o, copy = a_copy(dx, b)
            other(o, dx, copy.start)
    for r in range(ROUNDS):
        out_ref[pl.ds(r * cap * G + g, cap, stride=G), :] = sbuf[g, r]

    for d in (1, Z - 1):
        z_copy(d).wait_send()
    z_relay().wait_send()
    for e in range(Z):
        for j in rows:
            y_copy(e, j).wait_send()

    @pl.loop(0, UNITS)
    def _(s):
        for hop in range(2):
            f_copy(hop, s).wait_send()

    for dx in reversed(turns):
        for b in range(per_x):
            src = along(X - dx, b)

            def take(dx=dx, b=b, src=src):
                block = rbuf.at[src]
                remote(block, block, a_send.at[dx * per_x + b],
                       a_recv.at[dx * per_x + b], (src, f)).wait_recv()
                for r in range(ROUNDS):
                    out_ref[pl.ds(r * cap * G + src, cap, stride=G), :] = rbuf[src, r]

            other(src, dx, take)
    for dx in turns:
        for b in range(per_x):
            o, copy = a_copy(dx, b)
            other(o, dx, copy.wait_send)


def per_device(spectra, station_mask, owners):
    G = lax.axis_size("grp")
    F = lax.axis_size("freq")
    Y = F // Z
    cap = (2 * PAIRS + G - 1) // G
    capp = -(-cap // 8) * 8
    hbm = pl.BlockSpec(memory_space=pltpu.HBM)
    dma = pltpu.SemaphoreType.DMA
    vmem = pltpu.VMEM
    held = pl.pallas_call(
        functools.partial(kernel, (G, Y, cap, capp)),
        out_shape=jax.ShapeDtypeStruct((ROUNDS * cap * G, BINS), F32),
        in_specs=[hbm] * 3,
        out_specs=pl.BlockSpec(memory_space=vmem),
        scratch_shapes=[
            vmem((STA, 2, BINS), F32),
            vmem((1, STA), jnp.int32),
            vmem((ROUNDS, PAIRS), jnp.int32),
            vmem((ROUNDS, G * capp, PAIRS), BF16),
            vmem((2, F, BINS), F32),
            vmem((ROUNDS + 1, UNITS, Y // 2, 2, STA, BINS), F32),
            vmem((UNITS, Y * BINS, 2 * BINS), BF16),
            vmem((2 * ROUNDS * PAIRS, Y * BINS), BF16),
            vmem((2 * ROUNDS * PAIRS, 2 * BINS), F32),
            vmem((G, ROUNDS, cap, BINS), F32),
            vmem((G, ROUNDS, cap, BINS), F32),
            dma((3,)), dma((3,)), dma((3,)),
            dma((Z, Y)), dma((Z, Y)),
            dma((2, UNITS)), dma((2, UNITS)),
            dma((G,)), dma((G,)),
        ],
        compiler_params=pltpu.CompilerParams(
            collective_id=0, has_side_effects=True, vmem_limit_bytes=32 << 20),
    )(*(pltpu.with_memory_space_constraint(v, pltpu.HBM) for v in (spectra, station_mask.reshape(1, STA), owners.reshape(ROUNDS, PAIRS))))
    return held.reshape(1, ROUNDS, cap, G, BINS).transpose(0, 1, 3, 2, 4)


def solution(mesh):
    placed = (P("grp", None, "freq"), P("grp"), P("grp", None, None, None))
    return jax.shard_map(
        per_device,
        mesh=mesh,
        in_specs=placed,
        out_specs=P("grp", None, None, None, "freq"),
        check_vma=False,
    )
```

```python
import functools
import math

import jax
import jax.numpy as jnp
from jax import lax
from jax.experimental import pallas as pl
from jax.experimental.pallas import tpu as pltpu
from jax.sharding import PartitionSpec as P

BINS = 128
STA = 8
PAIRS = STA * STA
ROUNDS = 2
LAG = 4
Z = 4
CHIP_GROUPS = 6
UNITS = 2 * Z
PLACE = {1: 1, 3: 2, 2: 3}
MESH = pl.DeviceIdType.MESH
F32 = jnp.float32
BF16 = jnp.bfloat16


def split(v):
    hi = v.astype(BF16)
    return hi, (v - hi.astype(F32)).astype(BF16)


def trig(k, m, nf):
    angle = lax.rem(lax.rem(k * m, 2 * nf) + 2 * nf, 2 * nf).astype(F32) * (math.pi / nf)
    return jnp.cos(angle), jnp.sin(angle)


def kernel(
    dims, x_hbm, mask_hbm, owner_hbm, out_ref,
    xin, maskin, ownerin, place, phase, buf, tab, xb, acc, sbuf, rbuf,
    in_sem, z_send, z_recv, y_send, y_recv, f_send, f_recv, a_send, a_recv,
):
    G, Y, cap, capp = dims
    Q = Y // 2
    HALF = Q * BINS
    NF = Y * Z * BINS
    g = lax.axis_index("grp")
    f = lax.axis_index("freq")
    y = f // Z
    zh = lax.rem(f, Z)
    right = lax.rem(g + 1, G)
    per_x = CHIP_GROUPS if G % CHIP_GROUPS == 0 else 1
    X = G // per_x

    def zpeer(d):
        return (g, y * Z + lax.rem(zh + d, Z))

    def ypeer(d):
        return (g, lax.rem(y + d, Y) * Z + zh)

    turns = sorted(range(X), key=lambda dx: -min(dx, X - dx))
    mine = lax.rem(g, per_x)

    def along(dx, b):
        return lax.rem(g // per_x + dx, X) * per_x + b

    def other(o, dx, do):
        if dx == 0:
            pl.when(o != g)(do)
        else:
            do()

    loads = [
        pltpu.make_async_copy(a, b, in_sem.at[i])
        for i, (a, b) in enumerate(((x_hbm, xin), (mask_hbm, maskin), (owner_hbm, ownerin)))]
    for load in loads:
        load.start()

    barrier = pltpu.get_barrier_semaphore()

    def greet(peer):
        pl.semaphore_signal(barrier, inc=1, device_id=peer, device_id_type=MESH)

    greet(zpeer(1))
    greet(zpeer(Z - 1))

    @pl.loop(1, Y)
    def _(d):
        greet(ypeer(d))

    @pl.loop(1, G)
    def _(d):
        greet((lax.rem(g + d, G), f))


    for load in loads[:2]:
        load.wait()

    def column(row):
        n = row.shape[1]
        own = lax.broadcasted_iota(jnp.int32, (n, n), 0) == lax.broadcasted_iota(
            jnp.int32, (n, n), 1)
        return jnp.sum(jnp.where(own, row, 0.0), axis=1, keepdims=True)

    mask = column(maskin[...].astype(F32))
    buf[0, 0, 0, 0] = xin[:, 0, :] * mask
    buf[0, 0, 0, 1] = xin[:, 1, :] * mask
    def rel(i):
        return jnp.where(lax.rem(i, 2) == 1, (i + 1) // 2, lax.rem(Y - i // 2, Y))

    pl.semaphore_wait(barrier, 2 + (Y - 1) + (G - 1))

    def remote(src, dst, ssem, rsem, peer):
        return pltpu.make_async_remote_copy(
            src_ref=src, dst_ref=dst, send_sem=ssem, recv_sem=rsem,
            device_id=peer, device_id_type=MESH)

    def z_copy(d):
        return remote(buf.at[0, 0, 0], buf.at[0, 2 * PLACE[d], 0],
                      z_send.at[PLACE[d] - 1], z_recv.at[PLACE[d] - 1], zpeer(d))

    def z_relay():
        return remote(buf.at[0, 2 * PLACE[Z - 1], 0], buf.at[0, 2 * PLACE[2], 0],
                      z_send.at[2], z_recv.at[2], zpeer(Z - 1))

    def y_copy(e, j):
        i = 2 * j if j < Y // 2 else 2 * (Y - j) - 1
        return remote(buf.at[0, 2 * e, 0], buf.at[0, 2 * e + i // Q, i % Q],
                      y_send.at[e, j], y_recv.at[e, i], ypeer(j))

    rows = sorted(range(1, Y), key=lambda j: -min(j, Y - j))

    def f_copy(hop, s):
        return remote(buf.at[0, s], buf.at[hop + 1, s], f_send.at[hop, s],
                      f_recv.at[hop, s], (lax.rem(g + 1 + hop, G), f))

    def a_copy(dx, b):
        o = along(dx, b)
        return o, remote(sbuf.at[o], rbuf.at[g], a_send.at[dx * per_x + b],
                         a_recv.at[dx * per_x + mine], (o, f))

    z_copy(1).start()
    z_copy(Z - 1).start()
    for j in rows:
        y_copy(0, j).start()
    lag = f * BINS + lax.broadcasted_iota(jnp.int32, (1, BINS), 1) - NF // 2
    base_cos, base_sin = trig(lax.broadcasted_iota(jnp.int32, (BINS, 1), 0), lag, NF)
    first_cos, first_sin = trig(
        BINS * lax.broadcasted_iota(jnp.int32, (Y * Z, 1), 0), lag, NF)
    phase[0] = first_cos
    phase[1] = first_sin
    def table(s):
        e = s // 2
        d = jnp.where(e == 2, 3, jnp.where(e == 3, 2, e))
        col = lax.rem(zh + Z - d, Z)
        for q in range(Q):
            band = lax.rem(y + rel(lax.rem(s, 2) * Q + q), Y) * Z + col
            ec = phase[0, pl.ds(band, 1), :]
            es = phase[1, pl.ds(band, 1), :]
            c = base_cos * ec - base_sin * es
            n = -(base_sin * ec + base_cos * es)
            for at, v in ((q * BINS, c), (HALF + q * BINS, n)):
                hi, lo = split(v)
                tab[s, at:at + BINS, 0:BINS] = hi
                tab[s, at:at + BINS, BINS:2 * BINS] = lo

    pl.loop(0, UNITS // 2)(table)
    acc[...] = jnp.zeros_like(acc)
    z_copy(Z - 1).wait_recv()
    z_relay().start()
    for j in rows:
        y_copy(PLACE[Z - 1], j).start()
    z_copy(1).wait_recv()
    for j in rows:
        y_copy(PLACE[1], j).start()
    pl.loop(UNITS // 2, UNITS)(table)

    loads[2].wait()
    for r in range(ROUNDS):
        row = ownerin[r:r + 1, :].astype(F32)
        ahead = lax.broadcasted_iota(jnp.int32, (PAIRS, PAIRS), 0) < lax.broadcasted_iota(
            jnp.int32, (PAIRS, PAIRS), 1)
        same = jnp.where(ahead & (column(row) == row), 1.0, 0.0)
        slot = row * capp + jnp.sum(same, axis=0, keepdims=True)
        slots = lax.broadcasted_iota(jnp.int32, (G * capp, PAIRS), 0).astype(F32)
        place[r] = jnp.where(slots == slot, 1.0, 0.0).astype(BF16)


    def product(s):
        for q in range(Q):
            are = buf[0, s, q, 0]
            aim = buf[0, s, q, 1]
            for r in range(ROUNDS):
                bre = buf[r + 1, s, q, 0][None, :, :]
                bim = buf[r + 1, s, q, 1][None, :, :]
                re = are[:, None, :] * bre + aim[:, None, :] * bim
                im = aim[:, None, :] * bre - are[:, None, :] * bim
                for at, v in ((q * BINS, re), (HALF + q * BINS, im)):
                    hi, lo = split(v.reshape(PAIRS, BINS))
                    xb[2 * r * PAIRS:(2 * r + 1) * PAIRS, at:at + BINS] = hi
                    xb[(2 * r + 1) * PAIRS:(2 * r + 2) * PAIRS, at:at + BINS] = lo
        acc[...] += jnp.dot(xb[...], tab[s], preferred_element_type=F32)

    @pl.loop(0, UNITS + LAG + 1)
    def _(t):
        @pl.when(t == 2)
        def _():
            z_relay().wait_recv()
            for j in rows:
                y_copy(PLACE[2], j).start()

        @pl.when(t < UNITS)
        def _():
            e = t // 2
            for q in range(Q):
                def arrive(q=q):
                    band = buf.at[0, t, q]
                    remote(band, band, y_send.at[0, 0],
                           y_recv.at[e, lax.rem(t, 2) * Q + q], (right, f)).wait_recv()
                if q == 0:
                    pl.when(lax.rem(t, 2) == 1)(arrive)
                else:
                    arrive()
            f_copy(1, t).start()
            f_copy(0, t).start()

        @pl.when((t >= LAG) & (t != UNITS - 2))
        def _():
            u = t - LAG - jnp.where(t > UNITS - 2, 1, 0)
            f_copy(0, u).wait_recv()
            f_copy(1, u).wait_recv()
            product(u)

    for r in range(ROUNDS):
        top, low = 2 * r * PAIRS, (2 * r + 1) * PAIRS
        whole = (acc[top:low, 0:BINS] + acc[top:low, BINS:2 * BINS]
                 + acc[low:low + PAIRS, 0:BINS] + acc[low:low + PAIRS, BINS:2 * BINS])
        hi, lo = split(whole * (1.0 / math.sqrt(NF)))
        got = jnp.dot(place[r], hi, preferred_element_type=F32) + jnp.dot(
            place[r], lo, preferred_element_type=F32)
        sbuf[:, r] = got.reshape(G, capp, BINS)[:, 0:cap]
    for dx in turns:
        for b in range(per_x):
            o, copy = a_copy(dx, b)
            other(o, dx, copy.start)
    for r in range(ROUNDS):
        out_ref[pl.ds(r * cap * G + g, cap, stride=G), :] = sbuf[g, r]

    for d in (1, Z - 1):
        z_copy(d).wait_send()
    z_relay().wait_send()
    for e in range(Z):
        for j in rows:
            y_copy(e, j).wait_send()

    @pl.loop(0, UNITS)
    def _(s):
        for hop in range(2):
            f_copy(hop, s).wait_send()

    for dx in reversed(turns):
        for b in range(per_x):
            src = along(X - dx, b)

            def take(dx=dx, b=b, src=src):
                block = rbuf.at[src]
                remote(block, block, a_send.at[dx * per_x + b],
                       a_recv.at[dx * per_x + b], (src, f)).wait_recv()
                for r in range(ROUNDS):
                    out_ref[pl.ds(r * cap * G + src, cap, stride=G), :] = rbuf[src, r]

            other(src, dx, take)
    for dx in turns:
        for b in range(per_x):
            o, copy = a_copy(dx, b)
            other(o, dx, copy.wait_send)


def per_device(spectra, station_mask, owners):
    G = lax.axis_size("grp")
    F = lax.axis_size("freq")
    Y = F // Z
    cap = (2 * PAIRS + G - 1) // G
    capp = -(-cap // 8) * 8
    hbm = pl.BlockSpec(memory_space=pltpu.HBM)
    dma = pltpu.SemaphoreType.DMA
    vmem = pltpu.VMEM
    held = pl.pallas_call(
        functools.partial(kernel, (G, Y, cap, capp)),
        out_shape=jax.ShapeDtypeStruct((ROUNDS * cap * G, BINS), F32),
        in_specs=[hbm] * 3,
        out_specs=pl.BlockSpec(memory_space=vmem),
        scratch_shapes=[
            vmem((STA, 2, BINS), F32),
            vmem((1, STA), jnp.int32),
            vmem((ROUNDS, PAIRS), jnp.int32),
            vmem((ROUNDS, G * capp, PAIRS), BF16),
            vmem((2, F, BINS), F32),
            vmem((ROUNDS + 1, UNITS, Y // 2, 2, STA, BINS), F32),
            vmem((UNITS, Y * BINS, 2 * BINS), BF16),
            vmem((2 * ROUNDS * PAIRS, Y * BINS), BF16),
            vmem((2 * ROUNDS * PAIRS, 2 * BINS), F32),
            vmem((G, ROUNDS, cap, BINS), F32),
            vmem((G, ROUNDS, cap, BINS), F32),
            dma((3,)), dma((3,)), dma((3,)),
            dma((Z, Y)), dma((Z, Y)),
            dma((2, UNITS)), dma((2, UNITS)),
            dma((G,)), dma((G,)),
        ],
        compiler_params=pltpu.CompilerParams(
            collective_id=0, has_side_effects=True, vmem_limit_bytes=32 << 20),
    )(*(pltpu.with_memory_space_constraint(v, pltpu.HBM) for v in (spectra, station_mask.reshape(1, STA), owners.reshape(ROUNDS, PAIRS))))
    return held.reshape(1, ROUNDS, cap, G, BINS).transpose(0, 1, 3, 2, 4)


def solution(mesh):
    placed = (P("grp", None, "freq"), P("grp"), P("grp", None, None, None))
    return jax.shard_map(
        per_device,
        mesh=mesh,
        in_specs=placed,
        out_specs=P("grp", None, None, None, "freq"),
        check_vma=False,
    )
```
